32 devices in a mesh: seq: 8 (over y, x, core), ctx: 4 (over z).
Axes of the slice: x: 2, y: 2, z: 4, core: 2. Of those that a mesh axis runs over, the one named last changes fastest.
Arguments:
- tokens: bfloat16 [4096, 4096], P(('seq', 'ctx')), may hold values from -30 to 30
- modality: int32 [4096], P(('seq', 'ctx')), may hold values from 0 to 1, as said below
- keep_mask: int32 [4096], P(('seq', 'ctx')), may hold values from 0 to 1, as said below
- positions: int32 [4096], P(('seq', 'ctx')), may hold values from 0 to 4095
- modal_table: float32 [2, 4096], replicated, may hold values from -3 to 3
- norm_gain: float32 [4096], replicated, may hold values from 0.1 to 1.9
- norm_bias: float32 [4096], replicated, may hold values from -3 to 3
- qkv_weight: bfloat16 [3, 4096, 4096], P(None, None, 'seq'), may hold values from -1 to 1
- out_weight: bfloat16 [4096, 4096], P('seq'), may hold values from -0.09375 to 0.09375
- mask_token: float32 [4096], replicated, may hold values from -4 to 4
Outputs:
- encoded: float32 [4096, 4096], P(('seq', 'ctx'))
The draws below stay inside these ranges and needn't reach their ends.
Inputs may be any that keep to these rules, and one draw needn't show every extreme that they name: `modality`: 0 marks a video token and 1 a taxel token; ids come in aligned runs of 16 tokens; five eighths of the tokens are video, and all tokens of at least one device are taxel. `keep_mask`: exactly 256 video tokens and 768 taxel tokens are kept, 1024 in all; on at least one device every token is kept.
All inputs are finite; a program needn't handle non-finite values.
Results may differ from the reference program's by a relative error of at most 0.0075.
Values may be sent and summed in bfloat16 or wider, within the bound.
A program may use at most 64 MiB of HBM per device.

```python
import math
import jax
import jax.numpy as jnp
from jax import lax

HEADS = 32
HEAD_DIM = 128
D = 4096
TOK_DEV = 128
TOKENS = 4096
VISIBLE = 1024


def clip_layout(key):
    base_key = jax.random.fold_in(key, 5)
    key_dense, key_blocks, key_keep = jax.random.split(base_key, 3)
    blocks = TOKENS // 16
    per_shard = TOK_DEV // 16
    dense = jax.random.randint(key_dense, (), 0, TOKENS // TOK_DEV)
    block_index = jnp.arange(blocks, dtype=jnp.int32)
    in_dense = block_index // per_shard == dense
    order = jax.random.permutation(key_blocks, blocks).astype(jnp.int32)
    block_score = jnp.where(in_dense, -1 - block_index, order)
    block_rank = jnp.argsort(jnp.argsort(-block_score))
    video_block = block_rank < 5 * blocks // 8
    modality = jnp.repeat(jnp.where(video_block, 0, 1).astype(jnp.int32), 16)
    token_index = jnp.arange(TOKENS, dtype=jnp.int32)
    token_order = jax.random.permutation(key_keep, TOKENS).astype(jnp.int32)
    dense_token = token_index // TOK_DEV == dense
    token_score = jnp.where(dense_token, -1 - token_index, token_order)
    composite = modality * (2 * TOKENS) + token_score
    token_rank = jnp.argsort(jnp.argsort(composite))
    video_total = 5 * TOKENS // 8
    chosen = (token_rank < TOKENS // 16) | (token_rank >= video_total) & (token_rank < video_total + 3 * TOKENS // 16)
    return (modality, chosen.astype(jnp.int32))


def draw_modality(key, part):
    return clip_layout(key)[0]


def draw_keep_mask(key, part):
    return clip_layout(key)[1]


def draw_tokens(key, part):
    key_base, key_rows, key_cols = jax.random.split(jax.random.fold_in(key, 11), 3)
    row_scale = jnp.exp(jax.random.uniform(key_rows, (TOKENS, 1), jnp.float32, math.log(0.25), math.log(2.5)))
    col_scale = jnp.exp(jax.random.uniform(key_cols, (1, D), jnp.float32, math.log(0.3), math.log(3.0)))
    values = jnp.clip(jax.random.normal(key_base, (TOKENS, D), jnp.float32), -4.0, 4.0) * row_scale * col_scale
    return values.astype(jnp.bfloat16)


def draw_qkv_weight(key, part):
    key_base = jax.random.fold_in(jax.random.fold_in(key, 23), 0)
    lift = jnp.array([1.3, 1.3, 1.0], jnp.float32).reshape(3, 1, 1)
    values = jnp.clip(jax.random.normal(key_base, (3, D, D), jnp.float32), -4.0, 4.0) * D ** (-0.5) * lift
    return values.astype(jnp.bfloat16)


def with_ends(entries, rng, least, top_value):
    extent = entries.shape
    index_at = [jax.random.randint(jax.random.fold_in(rng, axis), (), 0, extent[axis]) for axis in range(len(extent))]
    entries = entries.at[tuple(index_at)].set(least)
    longest = extent.index(max(extent))
    index_at[longest] = (index_at[longest] + 1) % extent[longest]
    return entries.at[tuple(index_at)].set(top_value)


def level_of(key, shape, cuts, least, largest):
    level, own = 1.0, jax.random.fold_in(key, 6)
    for axis_at, blocks in cuts:
        heights = jnp.exp(jax.random.uniform(jax.random.fold_in(own, axis_at), (blocks,), jnp.float32, least / len(cuts), largest / len(cuts)))
        level = level * jnp.repeat(heights, shape[axis_at] // blocks).reshape([-1 if axis == axis_at else 1 for axis in range(len(shape))])
    return level


def normal_values(rng, dims, scale, most, cuts=(), held_as=jnp.bfloat16):
    factor_of = level_of(rng, dims, cuts, -0.22, 0.18) if cuts else 1.0
    result = jax.random.normal(rng, dims, jnp.float32) * scale * factor_of
    return jnp.minimum(jnp.maximum(result, -most), most).astype(held_as)


def setup_inputs(seed: int = 0) -> dict:
    seeds = jax.random.split(jax.random.key(seed), 11)
    tokens = draw_tokens(jax.random.fold_in(seeds[10], 71), 0)
    modality = draw_modality(jax.random.fold_in(seeds[10], 71), 0)
    keep_mask = draw_keep_mask(jax.random.fold_in(seeds[10], 71), 0)
    positions = with_ends(jax.random.randint(seeds[3], (TOKENS,), 0, TOKENS), jax.random.fold_in(seeds[3], 1), 0, TOKENS - 1).astype(jnp.int32)
    modal_table = normal_values(seeds[4], (2, D), 0.5, 3.0, (), jnp.float32)
    norm_gain = jnp.clip(1.0 + 0.18 * jax.random.normal(seeds[5], (D,), jnp.float32), 0.1, 1.9)
    norm_bias = normal_values(seeds[6], (D,), 0.5, 3.0, (), jnp.float32)
    qkv_weight = draw_qkv_weight(jax.random.fold_in(seeds[10], 71), 0)
    out_weight = normal_values(seeds[8], (D, D), D ** -0.5, 0.09375, ((0, 8),))
    mask_token = normal_values(seeds[9], (D,), 1.0, 4.0, (), jnp.float32)
    return {"tokens": tokens, "modality": modality, "keep_mask": keep_mask, "positions": positions, "modal_table": modal_table, "norm_gain": norm_gain, "norm_bias": norm_bias, "qkv_weight": qkv_weight, "out_weight": out_weight, "mask_token": mask_token}


EPSILON = 1e-06

def position_table(positions, feature_width):
    half_width = feature_width // 2
    frequency = jnp.exp(-math.log(10000.0) * jnp.arange(half_width, dtype=jnp.float32) / half_width)
    angles = positions.astype(jnp.float32)[:, None] * frequency[None, :]
    return jnp.concatenate([jnp.sin(angles), jnp.cos(angles)], axis=1)

def embed(tokens, modality, positions, modal_table):
    table_rows = jnp.where(modality[:, None] == 1, modal_table[1][None, :], modal_table[0][None, :])
    summed = tokens.astype(jnp.float32) + position_table(positions, tokens.shape[1]) + table_rows
    return summed.astype(jnp.bfloat16)

def layer_norm(embedded, norm_gain, norm_bias):
    values = embedded.astype(jnp.float32)
    row_mean = lax.optimization_barrier(jnp.mean(values, axis=1, keepdims=True))
    centered = values - row_mean
    row_var = lax.optimization_barrier(jnp.mean(centered * centered, axis=1, keepdims=True))
    return (centered * lax.rsqrt(row_var + EPSILON) * norm_gain + norm_bias).astype(jnp.bfloat16)

def reference(tokens, modality, keep_mask, positions, modal_table, norm_gain, norm_bias, qkv_weight, out_weight, mask_token):
    embedded = embed(tokens, modality, positions, modal_table)
    visible = jnp.nonzero(keep_mask == 1, size=VISIBLE, fill_value=0)[0].astype(jnp.int32)
    balanced = embedded[visible]
    normed = layer_norm(balanced, norm_gain, norm_bias)
    triple = jnp.einsum('rd,tdc->trc', normed.astype(jnp.float32), qkv_weight.astype(jnp.float32), precision=lax.Precision.HIGHEST).astype(jnp.bfloat16)
    queries = triple[0].reshape(VISIBLE, HEADS, HEAD_DIM).transpose(1, 0, 2)
    key_rows = triple[1].reshape(VISIBLE, HEADS, HEAD_DIM).transpose(1, 0, 2)
    values = triple[2].reshape(VISIBLE, HEADS, HEAD_DIM).transpose(1, 0, 2)
    score_scale = 1.0 / math.sqrt(HEAD_DIM)

    def one_head(parts):
        query_head, key_head, value_head = parts
        scores = jnp.dot(query_head, key_head.T, preferred_element_type=jnp.float32) * score_scale
        row_top = lax.optimization_barrier(jnp.max(scores, axis=1, keepdims=True))
        expanded = jnp.exp(scores - row_top)
        denominator = lax.optimization_barrier(jnp.sum(expanded, axis=1, keepdims=True))
        weights = expanded.astype(jnp.bfloat16)
        summed = jnp.dot(weights, value_head, preferred_element_type=jnp.float32)
        return (summed / denominator).astype(jnp.bfloat16)
    attended = lax.map(one_head, (queries, key_rows, values))
    attended = attended.transpose(1, 0, 2).reshape(VISIBLE, D)
    projected = jnp.dot(attended, out_weight, preferred_element_type=jnp.float32)
    finished = balanced.astype(jnp.float32) + projected
    filler = jnp.broadcast_to(mask_token[None, :], (TOKENS, D)).astype(jnp.float32)
    return filler.at[visible].set(finished)
```

```python
import math

import jax
import jax.numpy as jnp
from jax import lax
from jax.experimental import pallas as pl
from jax.experimental.pallas import tpu as pltpu
from jax.sharding import PartitionSpec as P

HEAD_DIM = 128


EPSILON = 1e-06
MESH = pl.DeviceIdType.MESH


def position_table(positions, feature_width):
    half_width = feature_width // 2
    frequency = jnp.exp(-math.log(10000.0) * jnp.arange(half_width, dtype=jnp.float32) / half_width)
    angles = positions.astype(jnp.float32)[:, None] * frequency[None, :]
    return jnp.concatenate([jnp.sin(angles), jnp.cos(angles)], axis=1)


def embed(tokens, modality, positions, modal_table):
    table_rows = jnp.where(modality[:, None] == 1, modal_table[1][None, :], modal_table[0][None, :])
    summed = tokens.astype(jnp.float32) + position_table(positions, tokens.shape[1]) + table_rows
    return summed.astype(jnp.bfloat16)


def layer_norm(embedded, norm_gain, norm_bias):
    values = embedded.astype(jnp.float32)
    row_mean = jnp.mean(values, axis=1, keepdims=True)
    centered = values - row_mean
    row_var = jnp.mean(centered * centered, axis=1, keepdims=True)
    return (centered * lax.rsqrt(row_var + EPSILON) * norm_gain + norm_bias).astype(jnp.bfloat16)


def everyone():
    seq_count, ctx_count = lax.axis_size("seq"), lax.axis_size("ctx")

    def place():
        return lax.axis_index("seq") * ctx_count + lax.axis_index("ctx")

    return seq_count * ctx_count, place, lambda j: {"seq": j // ctx_count, "ctx": lax.rem(j, ctx_count)}


def along(axis):
    return lax.axis_size(axis), lambda: lax.axis_index(axis), lambda j: {axis: j}


def same_parity():
    return (
        lax.axis_size("seq") // 2,
        lambda: lax.axis_index("seq") // 2,
        lambda j: {"seq": 2 * j + lax.rem(lax.axis_index("seq"), 2)},
    )


def siblings():
    return (
        2,
        lambda: lax.rem(lax.axis_index("seq"), 2),
        lambda j: {"seq": lax.axis_index("seq") // 2 * 2 + j},
    )


def exchange(x, group, source, target, out_shape, collective_id):
    count, place, device_of = group

    def kernel(x_ref, out_ref, send_sem, recv_sem, own_sem):
        me = place()
        barrier = pltpu.get_barrier_semaphore()

        def greet(step, carry):
            peer = lax.rem(me + step, count)
            pl.semaphore_signal(barrier, inc=1, device_id=device_of(peer), device_id_type=MESH)
            return carry

        def push(step):
            peer = lax.rem(me + step, count)
            return pltpu.make_async_remote_copy(
                src_ref=source(x_ref, peer),
                dst_ref=target(out_ref, me),
                send_sem=send_sem.at[step],
                recv_sem=recv_sem.at[step],
                device_id=device_of(peer),
                device_id_type=MESH,
            )

        def start(step, carry):
            push(step).start()
            return carry

        def finish(step, carry):
            push(step).wait()
            return carry

        lax.fori_loop(1, count, greet, 0)
        own = pltpu.make_async_copy(source(x_ref, me), target(out_ref, me), own_sem)
        own.start()
        pl.semaphore_wait(barrier, count - 1)
        lax.fori_loop(1, count, start, 0)
        lax.fori_loop(1, count, finish, 0)
        own.wait()

    return pl.pallas_call(
        kernel,
        out_shape=jax.ShapeDtypeStruct(out_shape, x.dtype),
        in_specs=[pl.BlockSpec(memory_space=pltpu.VMEM)],
        out_specs=pl.BlockSpec(memory_space=pltpu.VMEM),
        scratch_shapes=[
            pltpu.SemaphoreType.DMA((count,)),
            pltpu.SemaphoreType.DMA((count,)),
            pltpu.SemaphoreType.DMA,
        ],
        compiler_params=pltpu.CompilerParams(collective_id=collective_id, has_side_effects=True),
    )(x)


def part(ref, j):
    return ref.at[j]


def whole(ref, j):
    return ref


def attend(triple):
    _, heads, rows, _ = triple.shape
    block = min(rows, 256)
    score_scale = 1.0 / math.sqrt(HEAD_DIM)

    def kernel(q_ref, k_ref, v_ref, out_ref):
        scores = (
            lax.dot_general(
                q_ref[...], k_ref[...], (((1,), (1,)), ((), ())), preferred_element_type=jnp.float32
            )
            * score_scale
        )
        expanded = jnp.exp(scores - jnp.max(scores, axis=1, keepdims=True))
        total = jnp.sum(expanded, axis=1, keepdims=True)
        summed = jnp.dot(expanded.astype(jnp.bfloat16), v_ref[...], preferred_element_type=jnp.float32)
        out_ref[...] = (summed / total).astype(jnp.bfloat16)

    return pl.pallas_call(
        kernel,
        grid=(heads, rows // block),
        out_shape=jax.ShapeDtypeStruct((heads, rows, HEAD_DIM), jnp.bfloat16),
        in_specs=[
            pl.BlockSpec((None, None, block, HEAD_DIM), lambda h, i: (0, h, i, 0)),
            pl.BlockSpec((None, None, rows, HEAD_DIM), lambda h, i: (1, h, 0, 0)),
            pl.BlockSpec((None, None, rows, HEAD_DIM), lambda h, i: (2, h, 0, 0)),
        ],
        out_specs=pl.BlockSpec((None, block, HEAD_DIM), lambda h, i: (h, i, 0)),
    )(triple, triple, triple)


def attend_by_head(triple):
    _, group_rows, local_width = triple.shape
    ctx = along("ctx")
    count = ctx[0]
    width = local_width // count
    heads = width // HEAD_DIM
    gathered = exchange(
        triple,
        ctx,
        lambda ref, j: ref.at[:, :, pl.ds(pl.multiple_of(j * width, HEAD_DIM), width)],
        lambda ref, j: ref.at[:, pl.ds(pl.multiple_of(j * group_rows, group_rows), group_rows), :],
        (3, count * group_rows, width),
        3,
    )
    if heads == 1:
        split = gathered[:, None]
    else:
        split = jnp.transpose(
            gathered.reshape(3, count * group_rows, heads, HEAD_DIM), (0, 2, 1, 3)
        )
    done = attend(split)
    if heads == 1:
        done = done[0]
    else:
        done = jnp.transpose(done, (1, 0, 2)).reshape(count * group_rows, width)
    return exchange(
        done,
        ctx,
        lambda ref, j: ref.at[pl.ds(pl.multiple_of(j * group_rows, group_rows), group_rows), :],
        lambda ref, j: ref.at[:, pl.ds(pl.multiple_of(j * width, HEAD_DIM), width)],
        (group_rows, local_width),
        4,
    )


def attend_by_row(triple):
    queries, key_rows, values = (triple[0], triple[1], triple[2])
    group_rows, local_width = queries.shape
    heads_here = local_width // HEAD_DIM
    score_scale = 1.0 / math.sqrt(HEAD_DIM)
    both = lax.all_gather(jnp.stack([key_rows, values]), "ctx", axis=1, tiled=True)
    length = both.shape[1]
    query_heads = queries.reshape(group_rows, heads_here, HEAD_DIM)
    key_heads = both[0].reshape(length, heads_here, HEAD_DIM)
    value_heads = both[1].reshape(length, heads_here, HEAD_DIM)
    scores = (
        jnp.einsum("ghd,khd->hgk", query_heads, key_heads, preferred_element_type=jnp.float32)
        * score_scale
    )
    expanded = jnp.exp(scores - jnp.max(scores, axis=2, keepdims=True))
    total = jnp.sum(expanded, axis=2, keepdims=True)
    summed = jnp.einsum(
        "hgk,khd->hgd",
        expanded.astype(jnp.bfloat16),
        value_heads,
        preferred_element_type=jnp.float32,
    )
    attended = (summed / total).astype(jnp.bfloat16)
    return jnp.transpose(attended, (1, 0, 2)).reshape(group_rows, local_width)


def local(
    tokens,
    modality,
    keep_mask,
    positions,
    modal_table,
    norm_gain,
    norm_bias,
    qkv_weight,
    out_weight,
    mask_token,
):
    tok_rows, feature_width = tokens.shape
    seq_count = lax.axis_size("seq")
    ctx_count = lax.axis_size("ctx")
    devices = seq_count * ctx_count
    slot_count = (tok_rows + devices - 1) // devices
    capacity = devices * slot_count
    own_rows = tok_rows // 4
    my_index = lax.axis_index("seq") * ctx_count + lax.axis_index("ctx")
    visible = keep_mask == 1
    own_count = jnp.sum(keep_mask)
    counts = exchange(
        jnp.full((1, 128), own_count, jnp.int32), everyone(), whole, part, (devices, 1, 128), 0
    )[:, 0, 0]
    index = jnp.arange(devices, dtype=jnp.int32)
    starts = jnp.sum(jnp.where(index[None, :] < index[:, None], counts[None, :], 0), axis=1)
    my_start = jnp.sum(jnp.where(index < my_index, counts, 0))
    token_index = jnp.arange(tok_rows, dtype=jnp.int32)
    local_rank = (
        jnp.sum(jnp.where(token_index[None, :] <= token_index[:, None], keep_mask[None, :], 0), axis=1) - 1
    )
    global_rank = my_start + local_rank
    token_slot = jnp.where(
        visible, global_rank % devices * slot_count + local_rank // devices, capacity
    )
    slot_index = jnp.arange(capacity, dtype=jnp.int32)
    slot_of_token = (token_slot[:, None] == slot_index[None, :]).astype(jnp.bfloat16)
    slot_place = slot_index % slot_count
    source_start = jnp.repeat(starts, slot_count)
    source_count = jnp.repeat(counts, slot_count)
    offset = (my_index - source_start) % devices + devices * slot_place
    usable = offset < source_count
    slot_row = jnp.where(usable, (source_start + offset) // devices, own_rows)
    row_of_slot = (
        slot_row[:, None] == jnp.arange(own_rows, dtype=jnp.int32)[None, :]
    ).astype(jnp.bfloat16)

    embedded = embed(tokens, modality, positions, modal_table)

    def pick(choice, rows, side):
        return lax.dot_general(
            choice, rows, (((side,), (0,)), ((), ())), preferred_element_type=jnp.float32
        )

    outgoing = pick(slot_of_token, embedded, 0).astype(jnp.bfloat16)
    slots = (devices, slot_count, feature_width)
    arriving = exchange(outgoing.reshape(slots), everyone(), part, part, slots, 1)
    balanced = pick(row_of_slot, arriving.reshape(capacity, feature_width), 0)
    normed = layer_norm(balanced, norm_gain, norm_bias)
    group = exchange(normed, along("seq"), whole, part, (seq_count,) + normed.shape, 2)
    group = group.reshape(seq_count * own_rows, feature_width)
    triple = jnp.einsum(
        "rd,tdc->trc", group, qkv_weight, preferred_element_type=jnp.float32
    ).astype(jnp.bfloat16)
    if triple.shape[2] % (ctx_count * HEAD_DIM) == 0:
        attended = attend_by_head(triple)
    else:
        attended = attend_by_row(triple)
    shares = jnp.dot(attended, out_weight, preferred_element_type=jnp.float32).astype(jnp.bfloat16)
    shares = shares.reshape(seq_count, own_rows, feature_width)
    shares = exchange(shares, along("seq"), part, part, shares.shape, 5)
    projected = jnp.sum(shares.astype(jnp.float32), axis=0).astype(jnp.bfloat16)
    returning = pick(row_of_slot, projected, 1).astype(jnp.bfloat16)
    returned = exchange(returning.reshape(slots), everyone(), part, part, slots, 6)
    restored = pick(slot_of_token, returned.reshape(capacity, feature_width), 1)
    return jnp.where(visible[:, None], embedded.astype(jnp.float32) + restored, mask_token[None, :])


def solution(mesh):
    in_specs = (
        P(("seq", "ctx"), None),
        P(("seq", "ctx")),
        P(("seq", "ctx")),
        P(("seq", "ctx")),
        P(),
        P(),
        P(),
        P(None, None, "seq"),
        P("seq", None),
        P(),
    )
    out_specs = P(("seq", "ctx"), None)
    return jax.shard_map(local, mesh=mesh, in_specs=in_specs, out_specs=out_specs, check_vma=False)
```

```python
import math

import jax
import jax.numpy as jnp
from jax import lax
from jax.experimental import pallas as pl
from jax.experimental.pallas import tpu as pltpu
from jax.sharding import PartitionSpec as P

HEAD_DIM = 128


EPSILON = 1e-06
MESH = pl.DeviceIdType.MESH


def position_table(positions, feature_width):
    half_width = feature_width // 2
    frequency = jnp.exp(-math.log(10000.0) * jnp.arange(half_width, dtype=jnp.float32) / half_width)
    angles = positions.astype(jnp.float32)[:, None] * frequency[None, :]
    return jnp.concatenate([jnp.sin(angles), jnp.cos(angles)], axis=1)


def embed(tokens, modality, positions, modal_table):
    table_rows = jnp.where(modality[:, None] == 1, modal_table[1][None, :], modal_table[0][None, :])
    summed = tokens.astype(jnp.float32) + position_table(positions, tokens.shape[1]) + table_rows
    return summed.astype(jnp.bfloat16)


def layer_norm(embedded, norm_gain, norm_bias):
    values = embedded.astype(jnp.float32)
    row_mean = jnp.mean(values, axis=1, keepdims=True)
    centered = values - row_mean
    row_var = jnp.mean(centered * centered, axis=1, keepdims=True)
    return (centered * lax.rsqrt(row_var + EPSILON) * norm_gain + norm_bias).astype(jnp.bfloat16)


def everyone():
    seq_count, ctx_count = lax.axis_size("seq"), lax.axis_size("ctx")

    def place():
        return lax.axis_index("seq") * ctx_count + lax.axis_index("ctx")

    return seq_count * ctx_count, place, lambda j: {"seq": j // ctx_count, "ctx": lax.rem(j, ctx_count)}


def along(axis):
    return lax.axis_size(axis), lambda: lax.axis_index(axis), lambda j: {axis: j}


def exchange(x, group, source, target, out_shape, collective_id):
    count, place, device_of = group

    def kernel(x_ref, out_ref, send_sem, recv_sem, own_sem):
        me = place()
        barrier = pltpu.get_barrier_semaphore()

        def greet(step, carry):
            peer = lax.rem(me + step, count)
            pl.semaphore_signal(barrier, inc=1, device_id=device_of(peer), device_id_type=MESH)
            return carry

        def push(step):
            peer = lax.rem(me + step, count)
            return pltpu.make_async_remote_copy(
                src_ref=source(x_ref, peer),
                dst_ref=target(out_ref, me),
                send_sem=send_sem.at[step],
                recv_sem=recv_sem.at[step],
                device_id=device_of(peer),
                device_id_type=MESH,
            )

        def start(step, carry):
            push(step).start()
            return carry

        def finish(step, carry):
            push(step).wait()
            return carry

        lax.fori_loop(1, count, greet, 0)
        own = pltpu.make_async_copy(source(x_ref, me), target(out_ref, me), own_sem)
        own.start()
        pl.semaphore_wait(barrier, count - 1)
        lax.fori_loop(1, count, start, 0)
        lax.fori_loop(1, count, finish, 0)
        own.wait()

    return pl.pallas_call(
        kernel,
        out_shape=jax.ShapeDtypeStruct(out_shape, x.dtype),
        in_specs=[pl.BlockSpec(memory_space=pltpu.VMEM)],
        out_specs=pl.BlockSpec(memory_space=pltpu.VMEM),
        scratch_shapes=[
            pltpu.SemaphoreType.DMA((count,)),
            pltpu.SemaphoreType.DMA((count,)),
            pltpu.SemaphoreType.DMA,
        ],
        compiler_params=pltpu.CompilerParams(collective_id=collective_id, has_side_effects=True),
    )(x)


def flip(position, bit):
    return position + bit * (1 - 2 * lax.rem(position // bit, 2))


def greet_all(places):
    barrier = pltpu.get_barrier_semaphore()
    for place in places:
        pl.semaphore_signal(barrier, inc=1, device_id={"seq": place}, device_id_type=MESH)
    pl.semaphore_wait(barrier, len(places))


def gather_rows(x, collective_id):
    rows, width = x.shape
    half = rows // 2

    def kernel(x_ref, out_ref, send_sem, recv_sem, own_sem):
        me = lax.axis_index("seq")
        sibling, left, down = flip(me, 1), flip(me, 2), flip(me, 4)
        across = flip(left, 4)
        first, second = pl.ds(0, half), pl.ds(half, half)

        def push(sem, src, dst, place):
            return pltpu.make_async_remote_copy(
                src_ref=src,
                dst_ref=dst,
                send_sem=send_sem.at[sem],
                recv_sem=recv_sem.at[sem],
                device_id={"seq": place},
                device_id_type=MESH,
            )

        def own(sem, place):
            return push(sem, x_ref, out_ref.at[me], place)

        def relay(sem, origin, place):
            return push(sem, out_ref.at[origin], out_ref.at[origin], place)

        def relay_half(sem, origin, which, place):
            return push(sem, out_ref.at[origin, which], out_ref.at[origin, which], place)

        greet_all((sibling, left, down))
        to_left, to_down, to_sibling = own(1, left), own(2, down), own(0, sibling)
        to_left.start()
        to_down.start()
        to_sibling.start()
        keep = pltpu.make_async_copy(x_ref, out_ref.at[me], own_sem)
        keep.start()
        to_left.wait_recv()
        left_on = relay_half(3, left, first, down)
        left_on.start()
        left_over = relay(5, left, sibling)
        left_over.start()
        to_down.wait_recv()
        down_on = relay_half(4, down, second, left)
        down_on.start()
        down_over = relay(6, down, sibling)
        down_over.start()
        left_on.wait_recv()
        across_first = relay_half(7, across, first, sibling)
        across_first.start()
        down_on.wait_recv()
        across_second = relay_half(8, across, second, sibling)
        across_second.start()
        for copy in (to_sibling, left_over, down_over, across_first, across_second):
            copy.wait_recv()
        for copy in (to_left, to_down, to_sibling, left_on, left_over, down_on, down_over, across_first, across_second):
            copy.wait_send()
        keep.wait()

    return pl.pallas_call(
        kernel,
        out_shape=jax.ShapeDtypeStruct((8, rows, width), x.dtype),
        in_specs=[pl.BlockSpec(memory_space=pltpu.VMEM)],
        out_specs=pl.BlockSpec(memory_space=pltpu.VMEM),
        scratch_shapes=[
            pltpu.SemaphoreType.DMA((9,)),
            pltpu.SemaphoreType.DMA((9,)),
            pltpu.SemaphoreType.DMA,
        ],
        compiler_params=pltpu.CompilerParams(collective_id=collective_id, has_side_effects=True),
    )(x)


def scatter_sums(shares, collective_id):
    _, rows, width = shares.shape
    half = rows // 2

    def kernel(x_ref, out_ref, near, sums, from_left, from_down, last, passed, send_sem, recv_sem):
        me = lax.axis_index("seq")
        sibling, left, down = flip(me, 1), flip(me, 2), flip(me, 4)
        first, second = pl.ds(0, half), pl.ds(half, half)

        def push(sem, src, dst, place):
            copy = pltpu.make_async_remote_copy(
                src_ref=src,
                dst_ref=dst,
                send_sem=send_sem.at[sem],
                recv_sem=recv_sem.at[sem],
                device_id={"seq": place},
                device_id_type=MESH,
            )
            copy.start()
            return copy

        def at(place, which):
            place = flip(place, 2) if which % 2 else place
            return flip(place, 4) if which // 2 else place

        def wide(value):
            return value.astype(jnp.float32)

        greet_all((sibling, left, down))
        order = (3, 1, 2, 0)
        over = {q: push(q, x_ref.at[at(sibling, q)], near.at[q], sibling) for q in order}
        for q in order:
            over[q].wait_recv()
            sums[q] = (wide(x_ref[at(me, q)]) + wide(near[q])).astype(jnp.bfloat16)
            if q == 3:
                left_far = push(4, sums.at[3, first], from_left.at[1], left)
                down_far = push(5, sums.at[3, second], from_down.at[1], down)
            if q == 1:
                left_own = push(6, sums.at[1, first], from_left.at[0], left)
            if q == 2:
                down_own = push(7, sums.at[2, second], from_down.at[0], down)
        left_far.wait_recv()
        passed[0] = (wide(sums[2, :half]) + wide(from_left[1])).astype(jnp.bfloat16)
        down_last = push(8, passed.at[0], last.at[0], down)
        down_far.wait_recv()
        passed[1] = (wide(sums[1, half:]) + wide(from_down[1])).astype(jnp.bfloat16)
        left_last = push(9, passed.at[1], last.at[1], left)
        left_own.wait_recv()
        down_last.wait_recv()
        out_ref[:half] = (wide(sums[0, :half]) + wide(from_left[0]) + wide(last[0])).astype(jnp.bfloat16)
        down_own.wait_recv()
        left_last.wait_recv()
        out_ref[half:] = (wide(sums[0, half:]) + wide(from_down[0]) + wide(last[1])).astype(jnp.bfloat16)
        for copy in (*over.values(), left_far, down_far, left_own, down_own, down_last, left_last):
            copy.wait_send()

    return pl.pallas_call(
        kernel,
        out_shape=jax.ShapeDtypeStruct((rows, width), jnp.bfloat16),
        in_specs=[pl.BlockSpec(memory_space=pltpu.VMEM)],
        out_specs=pl.BlockSpec(memory_space=pltpu.VMEM),
        scratch_shapes=[
            pltpu.VMEM((4, rows, width), jnp.bfloat16),
            pltpu.VMEM((4, rows, width), jnp.bfloat16),
            pltpu.VMEM((2, half, width), jnp.bfloat16),
            pltpu.VMEM((2, half, width), jnp.bfloat16),
            pltpu.VMEM((2, half, width), jnp.bfloat16),
            pltpu.VMEM((2, half, width), jnp.bfloat16),
            pltpu.SemaphoreType.DMA((10,)),
            pltpu.SemaphoreType.DMA((10,)),
        ],
        compiler_params=pltpu.CompilerParams(collective_id=collective_id, has_side_effects=True),
    )(shares)


def part(ref, j):
    return ref.at[j]


def whole(ref, j):
    return ref


def attend(triple):
    _, heads, rows, _ = triple.shape
    block = min(rows, 256)
    score_scale = 1.0 / math.sqrt(HEAD_DIM)

    def kernel(q_ref, k_ref, v_ref, out_ref):
        scores = (
            lax.dot_general(
                q_ref[...], k_ref[...], (((1,), (1,)), ((), ())), preferred_element_type=jnp.float32
            )
            * score_scale
        )
        expanded = jnp.exp(scores - jnp.max(scores, axis=1, keepdims=True))
        total = jnp.sum(expanded, axis=1, keepdims=True)
        summed = jnp.dot(expanded.astype(jnp.bfloat16), v_ref[...], preferred_element_type=jnp.float32)
        out_ref[...] = (summed / total).astype(jnp.bfloat16)

    return pl.pallas_call(
        kernel,
        grid=(heads, rows // block),
        out_shape=jax.ShapeDtypeStruct((heads, rows, HEAD_DIM), jnp.bfloat16),
        in_specs=[
            pl.BlockSpec((None, None, block, HEAD_DIM), lambda h, i: (0, h, i, 0)),
            pl.BlockSpec((None, None, rows, HEAD_DIM), lambda h, i: (1, h, 0, 0)),
            pl.BlockSpec((None, None, rows, HEAD_DIM), lambda h, i: (2, h, 0, 0)),
        ],
        out_specs=pl.BlockSpec((None, block, HEAD_DIM), lambda h, i: (h, i, 0)),
    )(triple, triple, triple)


def attend_by_head(triple):
    _, group_rows, local_width = triple.shape
    ctx = along("ctx")
    count = ctx[0]
    width = local_width // count
    heads = width // HEAD_DIM
    gathered = exchange(
        triple,
        ctx,
        lambda ref, j: ref.at[:, :, pl.ds(pl.multiple_of(j * width, HEAD_DIM), width)],
        lambda ref, j: ref.at[:, pl.ds(pl.multiple_of(j * group_rows, group_rows), group_rows), :],
        (3, count * group_rows, width),
        3,
    )
    if heads == 1:
        split = gathered[:, None]
    else:
        split = jnp.transpose(
            gathered.reshape(3, count * group_rows, heads, HEAD_DIM), (0, 2, 1, 3)
        )
    done = attend(split)
    if heads == 1:
        done = done[0]
    else:
        done = jnp.transpose(done, (1, 0, 2)).reshape(count * group_rows, width)
    return exchange(
        done,
        ctx,
        lambda ref, j: ref.at[pl.ds(pl.multiple_of(j * group_rows, group_rows), group_rows), :],
        lambda ref, j: ref.at[:, pl.ds(pl.multiple_of(j * width, HEAD_DIM), width)],
        (group_rows, local_width),
        4,
    )


def attend_by_row(triple):
    queries, key_rows, values = (triple[0], triple[1], triple[2])
    group_rows, local_width = queries.shape
    heads_here = local_width // HEAD_DIM
    score_scale = 1.0 / math.sqrt(HEAD_DIM)
    both = lax.all_gather(jnp.stack([key_rows, values]), "ctx", axis=1, tiled=True)
    length = both.shape[1]
    query_heads = queries.reshape(group_rows, heads_here, HEAD_DIM)
    key_heads = both[0].reshape(length, heads_here, HEAD_DIM)
    value_heads = both[1].reshape(length, heads_here, HEAD_DIM)
    scores = (
        jnp.einsum("ghd,khd->hgk", query_heads, key_heads, preferred_element_type=jnp.float32)
        * score_scale
    )
    expanded = jnp.exp(scores - jnp.max(scores, axis=2, keepdims=True))
    total = jnp.sum(expanded, axis=2, keepdims=True)
    summed = jnp.einsum(
        "hgk,khd->hgd",
        expanded.astype(jnp.bfloat16),
        value_heads,
        preferred_element_type=jnp.float32,
    )
    attended = (summed / total).astype(jnp.bfloat16)
    return jnp.transpose(attended, (1, 0, 2)).reshape(group_rows, local_width)


def local(
    tokens,
    modality,
    keep_mask,
    positions,
    modal_table,
    norm_gain,
    norm_bias,
    qkv_weight,
    out_weight,
    mask_token,
):
    tok_rows, feature_width = tokens.shape
    seq_count = lax.axis_size("seq")
    ctx_count = lax.axis_size("ctx")
    devices = seq_count * ctx_count
    slot_count = (tok_rows + devices - 1) // devices
    capacity = devices * slot_count
    own_rows = tok_rows // 4
    my_index = lax.axis_index("seq") * ctx_count + lax.axis_index("ctx")
    visible = keep_mask == 1
    own_count = jnp.sum(keep_mask)
    counts = exchange(
        jnp.full((1, 128), own_count, jnp.int32), everyone(), whole, part, (devices, 1, 128), 0
    )[:, 0, 0]
    index = jnp.arange(devices, dtype=jnp.int32)
    starts = jnp.sum(jnp.where(index[None, :] < index[:, None], counts[None, :], 0), axis=1)
    my_start = jnp.sum(jnp.where(index < my_index, counts, 0))
    token_index = jnp.arange(tok_rows, dtype=jnp.int32)
    local_rank = (
        jnp.sum(jnp.where(token_index[None, :] <= token_index[:, None], keep_mask[None, :], 0), axis=1) - 1
    )
    global_rank = my_start + local_rank
    token_slot = jnp.where(
        visible, global_rank % devices * slot_count + local_rank // devices, capacity
    )
    slot_index = jnp.arange(capacity, dtype=jnp.int32)
    slot_of_token = (token_slot[:, None] == slot_index[None, :]).astype(jnp.bfloat16)
    slot_place = slot_index % slot_count
    source_start = jnp.repeat(starts, slot_count)
    source_count = jnp.repeat(counts, slot_count)
    offset = (my_index - source_start) % devices + devices * slot_place
    usable = offset < source_count
    slot_row = jnp.where(usable, (source_start + offset) // devices, own_rows)
    row_of_slot = (
        slot_row[:, None] == jnp.arange(own_rows, dtype=jnp.int32)[None, :]
    ).astype(jnp.bfloat16)

    embedded = embed(tokens, modality, positions, modal_table)

    def pick(choice, rows, side):
        return lax.dot_general(
            choice, rows, (((side,), (0,)), ((), ())), preferred_element_type=jnp.float32
        )

    outgoing = pick(slot_of_token, embedded, 0).astype(jnp.bfloat16)
    slots = (devices, slot_count, feature_width)
    arriving = exchange(outgoing.reshape(slots), everyone(), part, part, slots, 1)
    balanced = pick(row_of_slot, arriving.reshape(capacity, feature_width), 0)
    normed = layer_norm(balanced, norm_gain, norm_bias)
    if seq_count == 8:
        group = gather_rows(normed, 2)
    else:
        group = exchange(normed, along("seq"), whole, part, (seq_count,) + normed.shape, 2)
    group = group.reshape(seq_count * own_rows, feature_width)
    triple = jnp.einsum(
        "rd,tdc->trc", group, qkv_weight, preferred_element_type=jnp.float32
    ).astype(jnp.bfloat16)
    if triple.shape[2] % (ctx_count * HEAD_DIM) == 0:
        attended = attend_by_head(triple)
    else:
        attended = attend_by_row(triple)
    shares = jnp.dot(attended, out_weight, preferred_element_type=jnp.float32).astype(jnp.bfloat16)
    shares = shares.reshape(seq_count, own_rows, feature_width)
    if seq_count == 8:
        projected = scatter_sums(shares, 5)
    else:
        shares = exchange(shares, along("seq"), part, part, shares.shape, 5)
        projected = jnp.sum(shares.astype(jnp.float32), axis=0).astype(jnp.bfloat16)
    returning = pick(row_of_slot, projected, 1).astype(jnp.bfloat16)
    returned = exchange(returning.reshape(slots), everyone(), part, part, slots, 6)
    restored = pick(slot_of_token, returned.reshape(capacity, feature_width), 1)
    return jnp.where(visible[:, None], embedded.astype(jnp.float32) + restored, mask_token[None, :])


def solution(mesh):
    in_specs = (
        P(("seq", "ctx"), None),
        P(("seq", "ctx")),
        P(("seq", "ctx")),
        P(("seq", "ctx")),
        P(),
        P(),
        P(),
        P(None, None, "seq"),
        P("seq", None),
        P(),
    )
    out_specs = P(("seq", "ctx"), None)
    return jax.shard_map(local, mesh=mesh, in_specs=in_specs, out_specs=out_specs, check_vma=False)
```

```python
import math

import jax
import jax.numpy as jnp
from jax import lax
from jax.experimental import pallas as pl
from jax.experimental.pallas import tpu as pltpu
from jax.sharding import PartitionSpec as P

HEAD_DIM = 128


EPSILON = 1e-06
MESH = pl.DeviceIdType.MESH


def position_table(positions, feature_width):
    half_width = feature_width // 2
    frequency = jnp.exp(-math.log(10000.0) * jnp.arange(half_width, dtype=jnp.float32) / half_width)
    angles = positions.astype(jnp.float32)[:, None] * frequency[None, :]
    return jnp.concatenate([jnp.sin(angles), jnp.cos(angles)], axis=1)


def embed(tokens, modality, positions, modal_table):
    table_rows = jnp.where(modality[:, None] == 1, modal_table[1][None, :], modal_table[0][None, :])
    summed = tokens.astype(jnp.float32) + position_table(positions, tokens.shape[1]) + table_rows
    return summed.astype(jnp.bfloat16)


def layer_norm(embedded, norm_gain, norm_bias):
    values = embedded.astype(jnp.float32)
    row_mean = jnp.mean(values, axis=1, keepdims=True)
    centered = values - row_mean
    row_var = jnp.mean(centered * centered, axis=1, keepdims=True)
    return (centered * lax.rsqrt(row_var + EPSILON) * norm_gain + norm_bias).astype(jnp.bfloat16)


def everyone():
    seq_count, ctx_count = lax.axis_size("seq"), lax.axis_size("ctx")

    def place():
        return lax.axis_index("seq") * ctx_count + lax.axis_index("ctx")

    return seq_count * ctx_count, place, lambda j: {"seq": j // ctx_count, "ctx": lax.rem(j, ctx_count)}


def along(axis):
    return lax.axis_size(axis), lambda: lax.axis_index(axis), lambda j: {axis: j}


def exchange(x, group, source, target, out_shape, collective_id):
    count, place, device_of = group

    def kernel(x_ref, out_ref, send_sem, recv_sem, own_sem):
        me = place()
        barrier = pltpu.get_barrier_semaphore()

        def greet(step, carry):
            peer = lax.rem(me + step, count)
            pl.semaphore_signal(barrier, inc=1, device_id=device_of(peer), device_id_type=MESH)
            return carry

        def push(step):
            peer = lax.rem(me + step, count)
            return pltpu.make_async_remote_copy(
                src_ref=source(x_ref, peer),
                dst_ref=target(out_ref, me),
                send_sem=send_sem.at[step],
                recv_sem=recv_sem.at[step],
                device_id=device_of(peer),
                device_id_type=MESH,
            )

        def start(step, carry):
            push(step).start()
            return carry

        def finish(step, carry):
            push(step).wait()
            return carry

        lax.fori_loop(1, count, greet, 0)
        own = pltpu.make_async_copy(source(x_ref, me), target(out_ref, me), own_sem)
        own.start()
        pl.semaphore_wait(barrier, count - 1)
        lax.fori_loop(1, count, start, 0)
        lax.fori_loop(1, count, finish, 0)
        own.wait()

    return pl.pallas_call(
        kernel,
        out_shape=jax.ShapeDtypeStruct(out_shape, x.dtype),
        in_specs=[pl.BlockSpec(memory_space=pltpu.VMEM)],
        out_specs=pl.BlockSpec(memory_space=pltpu.VMEM),
        scratch_shapes=[
            pltpu.SemaphoreType.DMA((count,)),
            pltpu.SemaphoreType.DMA((count,)),
            pltpu.SemaphoreType.DMA,
        ],
        compiler_params=pltpu.CompilerParams(collective_id=collective_id, has_side_effects=True),
    )(x)


CHUNKS = 4


def remote(src, dst, sems, at, device):
    send_sem, recv_sem = sems
    return pltpu.make_async_remote_copy(
        src_ref=src,
        dst_ref=dst,
        send_sem=send_sem.at[at],
        recv_sem=recv_sem.at[at],
        device_id=device,
        device_id_type=MESH,
    )


def aligned(start, size):
    return pl.ds(pl.multiple_of(start * size, size), size)


def greet_line_and_plane(seq_count, ctx_count):
    me, level = lax.axis_index("seq"), lax.axis_index("ctx")
    barrier = pltpu.get_barrier_semaphore()
    for step in range(1, seq_count):
        peer = {"seq": lax.rem(me + step, seq_count)}
        pl.semaphore_signal(barrier, inc=1, device_id=peer, device_id_type=MESH)
    for step in range(1, ctx_count):
        peer = {"ctx": lax.rem(level + step, ctx_count)}
        pl.semaphore_signal(barrier, inc=1, device_id=peer, device_id_type=MESH)
    pl.semaphore_wait(barrier, seq_count + ctx_count - 2)


def regrouping(capacity, outer, inner, slot_count):
    row = lax.broadcasted_iota(jnp.int32, (capacity, capacity), 0)
    column = lax.broadcasted_iota(jnp.int32, (capacity, capacity), 1)
    first = row // (inner * slot_count)
    second = row // slot_count % inner
    wanted = (second * outer + first) * slot_count + row % slot_count
    return (column == wanted).astype(jnp.bfloat16)


def moved(choice, rows):
    return jnp.dot(choice, rows, preferred_element_type=jnp.float32).astype(jnp.bfloat16)


def spread_rows(outgoing, choice, slot_count, collective_id):
    capacity, width = outgoing.shape
    rows = choice.shape[0]
    half = rows // 2
    seq_count, ctx_count = lax.axis_size("seq"), lax.axis_size("ctx")
    line_rows, plane_rows = capacity // ctx_count, capacity // seq_count
    part_width = width // CHUNKS

    def kernel(x_ref, choice_ref, out_ref, mid, ordered, arrived, zs, zr, ps, pr, gs, gr, own_sem, own_sems):
        me, level = lax.axis_index("seq"), lax.axis_index("ctx")
        sibling, left, down = flip(me, 1), flip(me, 2), flip(me, 4)
        across = flip(left, 4)
        all_rows, first, second = pl.ds(0, rows), pl.ds(0, half), pl.ds(half, half)
        along_line, over_plane, gathering = (zs, zr), (ps, pr), (gs, gr)

        def cols(k):
            return pl.ds(k * part_width, part_width)

        def line(k, step):
            peer = lax.rem(level + step, ctx_count)
            src = x_ref.at[aligned(peer, line_rows), cols(k)]
            dst = mid.at[aligned(level, line_rows), cols(k)]
            return remote(src, dst, along_line, (k, step), {"ctx": peer})

        def plane(k, step):
            peer = lax.rem(me + step, seq_count)
            src = ordered.at[aligned(peer, plane_rows), cols(k)]
            dst = arrived.at[aligned(me, plane_rows), cols(k)]
            return remote(src, dst, over_plane, (k, step), {"seq": peer})

        def plane_own(k):
            here = aligned(me, plane_rows)
            return pltpu.make_async_copy(ordered.at[here, cols(k)], arrived.at[here, cols(k)], own_sems.at[k])

        moves = (
            (me, all_rows, sibling),
            (me, all_rows, left),
            (me, all_rows, down),
            (left, first, down),
            (down, second, left),
            (left, all_rows, sibling),
            (down, all_rows, sibling),
            (across, first, sibling),
            (across, second, sibling),
        )

        def hand(k, at):
            origin, which, place = moves[at]
            ref = out_ref.at[origin, which, cols(k)]
            return remote(ref, ref, gathering, (k, at), {"seq": place})

        greet_line_and_plane(seq_count, ctx_count)
        for k in range(CHUNKS):
            for step in range(1, ctx_count):
                line(k, step).start()
        here = aligned(level, line_rows)
        own = pltpu.make_async_copy(x_ref.at[here], mid.at[here], own_sem)
        own.start()
        regroup = regrouping(capacity, seq_count, ctx_count, slot_count)
        own.wait()
        for turn in range(CHUNKS + 3):
            k = turn - 3
            if 0 <= k < CHUNKS:
                hand(k, 3).wait_recv()
                hand(k, 7).start()
                hand(k, 4).wait_recv()
                hand(k, 8).start()
            k = turn - 2
            if 0 <= k < CHUNKS:
                hand(k, 1).wait_recv()
                hand(k, 3).start()
                hand(k, 5).start()
                hand(k, 2).wait_recv()
                hand(k, 4).start()
                hand(k, 6).start()
            k = turn - 1
            if 0 <= k < CHUNKS:
                for step in range(1, seq_count):
                    plane(k, step).wait_recv()
                plane_own(k).wait()
                out_ref[me, :, cols(k)] = moved(choice_ref[...], arrived[:, cols(k)])
                for at in (1, 2, 0):
                    hand(k, at).start()
            k = turn
            if k < CHUNKS:
                for step in range(1, ctx_count):
                    line(k, step).wait_recv()
                ordered[:, cols(k)] = moved(regroup, mid[:, cols(k)])
                for step in range(1, seq_count):
                    plane(k, step).start()
                plane_own(k).start()
        for k in range(CHUNKS):
            for at in (0, 5, 6, 7, 8):
                hand(k, at).wait_recv()
            for at in range(9):
                hand(k, at).wait_send()
            for step in range(1, seq_count):
                plane(k, step).wait_send()
            for step in range(1, ctx_count):
                line(k, step).wait_send()

    dma = pltpu.SemaphoreType.DMA
    return pl.pallas_call(
        kernel,
        out_shape=jax.ShapeDtypeStruct((seq_count, rows, width), jnp.bfloat16),
        in_specs=[pl.BlockSpec(memory_space=pltpu.VMEM)] * 2,
        out_specs=pl.BlockSpec(memory_space=pltpu.VMEM),
        scratch_shapes=[pltpu.VMEM((capacity, width), jnp.bfloat16)] * 3
        + [dma((CHUNKS, ctx_count))] * 2
        + [dma((CHUNKS, seq_count))] * 2
        + [dma((CHUNKS, 9))] * 2
        + [dma, dma((CHUNKS,))],
        compiler_params=pltpu.CompilerParams(collective_id=collective_id, has_side_effects=True),
    )(outgoing, choice)


def flip(position, bit):
    return position + bit * (1 - 2 * lax.rem(position // bit, 2))


def return_rows(attended, out_weight, choice, slot_count, collective_id):
    width = out_weight.shape[1]
    capacity, rows = choice.shape
    half = rows // 2
    seq_count, ctx_count = lax.axis_size("seq"), lax.axis_size("ctx")
    line_rows, plane_rows = capacity // ctx_count, capacity // seq_count
    part_width = width // CHUNKS

    def kernel(
        x_ref, w_ref, choice_ref, out_ref, shares, near, sums, from_left, from_down, last, passed, total,
        sorted_rows, arrived, ordered, ss, sr, ps, pr, zs, zr, own_sems, line_sems,
    ):
        me, level = lax.axis_index("seq"), lax.axis_index("ctx")
        sibling, left, down = flip(me, 1), flip(me, 2), flip(me, 4)
        first, second = pl.ds(0, half), pl.ds(half, half)
        summing, over_plane, along_line = (ss, sr), (ps, pr), (zs, zr)

        def cols(k):
            return pl.ds(k * part_width, part_width)

        def at(place, which):
            place = flip(place, 2) if which % 2 else place
            return flip(place, 4) if which // 2 else place

        def over(k, q):
            src = shares.at[aligned(at(sibling, q), rows), cols(k)]
            return remote(src, near.at[q, :, cols(k)], summing, (k, q), {"seq": sibling})

        def far(k, which):
            if which == 0:
                return remote(sums.at[3, first, cols(k)], from_left.at[1, :, cols(k)], summing, (k, 4), {"seq": left})
            if which == 1:
                return remote(sums.at[3, second, cols(k)], from_down.at[1, :, cols(k)], summing, (k, 5), {"seq": down})
            if which == 2:
                return remote(sums.at[1, first, cols(k)], from_left.at[0, :, cols(k)], summing, (k, 6), {"seq": left})
            if which == 3:
                return remote(sums.at[2, second, cols(k)], from_down.at[0, :, cols(k)], summing, (k, 7), {"seq": down})
            if which == 4:
                return remote(passed.at[0, :, cols(k)], last.at[0, :, cols(k)], summing, (k, 8), {"seq": down})
            return remote(passed.at[1, :, cols(k)], last.at[1, :, cols(k)], summing, (k, 9), {"seq": left})

        def plane(k, step):
            peer = lax.rem(me + step, seq_count)
            src = sorted_rows.at[aligned(peer, plane_rows), cols(k)]
            dst = arrived.at[aligned(me, plane_rows), cols(k)]
            return remote(src, dst, over_plane, (k, step), {"seq": peer})

        def plane_own(k):
            here = aligned(me, plane_rows)
            return pltpu.make_async_copy(sorted_rows.at[here, cols(k)], arrived.at[here, cols(k)], own_sems.at[k])

        def line(k, step):
            peer = lax.rem(level + step, ctx_count)
            src = ordered.at[aligned(peer, line_rows), cols(k)]
            dst = out_ref.at[aligned(level, line_rows), cols(k)]
            return remote(src, dst, along_line, (k, step), {"ctx": peer})

        def line_own(k):
            here = aligned(level, line_rows)
            return pltpu.make_async_copy(ordered.at[here, cols(k)], out_ref.at[here, cols(k)], line_sems.at[k])

        def wide(value):
            return value.astype(jnp.float32)

        def narrow(value):
            return value.astype(jnp.bfloat16)

        greet_line_and_plane(seq_count, ctx_count)
        regroup = regrouping(capacity, ctx_count, seq_count, slot_count)
        order = (3, 1, 2, 0)
        for turn in range(CHUNKS + 4):
            k = turn - 4
            if 0 <= k < CHUNKS:
                for step in range(1, seq_count):
                    plane(k, step).wait_recv()
                plane_own(k).wait()
                ordered[:, cols(k)] = moved(regroup, arrived[:, cols(k)])
                for step in range(1, ctx_count):
                    line(k, step).start()
                line_own(k).start()
            k = turn - 3
            if 0 <= k < CHUNKS:
                c = cols(k)
                far(k, 2).wait_recv()
                far(k, 4).wait_recv()
                total[:half, c] = narrow(wide(sums[0, :half, c]) + wide(from_left[0, :, c]) + wide(last[0, :, c]))
                far(k, 3).wait_recv()
                far(k, 5).wait_recv()
                total[half:, c] = narrow(wide(sums[0, half:, c]) + wide(from_down[0, :, c]) + wide(last[1, :, c]))
                sorted_rows[:, c] = moved(choice_ref[...], total[:, c])
                for step in range(1, seq_count):
                    plane(k, step).start()
                plane_own(k).start()
            k = turn - 2
            if 0 <= k < CHUNKS:
                c = cols(k)
                far(k, 0).wait_recv()
                passed[0, :, c] = narrow(wide(sums[2, :half, c]) + wide(from_left[1, :, c]))
                far(k, 4).start()
                far(k, 1).wait_recv()
                passed[1, :, c] = narrow(wide(sums[1, half:, c]) + wide(from_down[1, :, c]))
                far(k, 5).start()
            k = turn - 1
            if 0 <= k < CHUNKS:
                c = cols(k)
                for q in order:
                    over(k, q).wait_recv()
                    mine = shares[aligned(at(me, q), rows), c]
                    sums[q, :, c] = narrow(wide(mine) + wide(near[q, :, c]))
                    if q == 3:
                        far(k, 0).start()
                        far(k, 1).start()
                    if q == 1:
                        far(k, 2).start()
                    if q == 2:
                        far(k, 3).start()
            k = turn
            if k < CHUNKS:
                shares[:, cols(k)] = moved(x_ref[...], w_ref[:, cols(k)])
                for q in order:
                    over(k, q).start()
        for k in range(CHUNKS):
            for step in range(1, ctx_count):
                line(k, step).wait()
            line_own(k).wait()
            for step in range(1, seq_count):
                plane(k, step).wait_send()
            for q in order:
                over(k, q).wait_send()
            for which in range(6):
                far(k, which).wait_send()

    dma = pltpu.SemaphoreType.DMA
    bf16 = jnp.bfloat16
    return pl.pallas_call(
        kernel,
        out_shape=jax.ShapeDtypeStruct((capacity, width), bf16),
        in_specs=[pl.BlockSpec(memory_space=pltpu.VMEM)] * 3,
        out_specs=pl.BlockSpec(memory_space=pltpu.VMEM),
        scratch_shapes=[pltpu.VMEM((seq_count * rows, width), bf16)]
        + [pltpu.VMEM((4, rows, width), bf16)] * 2
        + [pltpu.VMEM((2, half, width), bf16)] * 4
        + [pltpu.VMEM((rows, width), bf16)]
        + [pltpu.VMEM((capacity, width), bf16)] * 3
        + [dma((CHUNKS, 10))] * 2
        + [dma((CHUNKS, seq_count))] * 2
        + [dma((CHUNKS, ctx_count))] * 2
        + [dma((CHUNKS,))] * 2,
        compiler_params=pltpu.CompilerParams(collective_id=collective_id, has_side_effects=True),
    )(attended, out_weight, choice)


def part(ref, j):
    return ref.at[j]


def whole(ref, j):
    return ref


def attend(triple):
    _, heads, rows, _ = triple.shape
    block = min(rows, 256)
    score_scale = 1.0 / math.sqrt(HEAD_DIM)

    def kernel(q_ref, k_ref, v_ref, out_ref):
        scores = (
            lax.dot_general(
                q_ref[...], k_ref[...], (((1,), (1,)), ((), ())), preferred_element_type=jnp.float32
            )
            * score_scale
        )
        expanded = jnp.exp(scores - jnp.max(scores, axis=1, keepdims=True))
        total = jnp.sum(expanded, axis=1, keepdims=True)
        summed = jnp.dot(expanded.astype(jnp.bfloat16), v_ref[...], preferred_element_type=jnp.float32)
        out_ref[...] = (summed / total).astype(jnp.bfloat16)

    return pl.pallas_call(
        kernel,
        grid=(heads, rows // block),
        out_shape=jax.ShapeDtypeStruct((heads, rows, HEAD_DIM), jnp.bfloat16),
        in_specs=[
            pl.BlockSpec((None, None, block, HEAD_DIM), lambda h, i: (0, h, i, 0)),
            pl.BlockSpec((None, None, rows, HEAD_DIM), lambda h, i: (1, h, 0, 0)),
            pl.BlockSpec((None, None, rows, HEAD_DIM), lambda h, i: (2, h, 0, 0)),
        ],
        out_specs=pl.BlockSpec((None, block, HEAD_DIM), lambda h, i: (h, i, 0)),
    )(triple, triple, triple)


def attend_by_head(triple):
    _, group_rows, local_width = triple.shape
    ctx = along("ctx")
    count = ctx[0]
    width = local_width // count
    heads = width // HEAD_DIM
    gathered = exchange(
        triple,
        ctx,
        lambda ref, j: ref.at[:, :, pl.ds(pl.multiple_of(j * width, HEAD_DIM), width)],
        lambda ref, j: ref.at[:, pl.ds(pl.multiple_of(j * group_rows, group_rows), group_rows), :],
        (3, count * group_rows, width),
        3,
    )
    if heads == 1:
        split = gathered[:, None]
    else:
        split = jnp.transpose(
            gathered.reshape(3, count * group_rows, heads, HEAD_DIM), (0, 2, 1, 3)
        )
    done = attend(split)
    if heads == 1:
        done = done[0]
    else:
        done = jnp.transpose(done, (1, 0, 2)).reshape(count * group_rows, width)
    return exchange(
        done,
        ctx,
        lambda ref, j: ref.at[pl.ds(pl.multiple_of(j * group_rows, group_rows), group_rows), :],
        lambda ref, j: ref.at[:, pl.ds(pl.multiple_of(j * width, HEAD_DIM), width)],
        (group_rows, local_width),
        4,
    )


def attend_by_row(triple):
    queries, key_rows, values = (triple[0], triple[1], triple[2])
    group_rows, local_width = queries.shape
    heads_here = local_width // HEAD_DIM
    score_scale = 1.0 / math.sqrt(HEAD_DIM)
    both = lax.all_gather(jnp.stack([key_rows, values]), "ctx", axis=1, tiled=True)
    length = both.shape[1]
    query_heads = queries.reshape(group_rows, heads_here, HEAD_DIM)
    key_heads = both[0].reshape(length, heads_here, HEAD_DIM)
    value_heads = both[1].reshape(length, heads_here, HEAD_DIM)
    scores = (
        jnp.einsum("ghd,khd->hgk", query_heads, key_heads, preferred_element_type=jnp.float32)
        * score_scale
    )
    expanded = jnp.exp(scores - jnp.max(scores, axis=2, keepdims=True))
    total = jnp.sum(expanded, axis=2, keepdims=True)
    summed = jnp.einsum(
        "hgk,khd->hgd",
        expanded.astype(jnp.bfloat16),
        value_heads,
        preferred_element_type=jnp.float32,
    )
    attended = (summed / total).astype(jnp.bfloat16)
    return jnp.transpose(attended, (1, 0, 2)).reshape(group_rows, local_width)


def local(
    tokens,
    modality,
    keep_mask,
    positions,
    modal_table,
    norm_gain,
    norm_bias,
    qkv_weight,
    out_weight,
    mask_token,
):
    tok_rows, feature_width = tokens.shape
    seq_count = lax.axis_size("seq")
    ctx_count = lax.axis_size("ctx")
    devices = seq_count * ctx_count
    slot_count = (tok_rows + devices - 1) // devices
    capacity = devices * slot_count
    own_rows = tok_rows // 4
    my_index = lax.axis_index("seq") * ctx_count + lax.axis_index("ctx")
    visible = keep_mask == 1
    own_count = jnp.sum(keep_mask)
    counts = exchange(
        jnp.full((1, 128), own_count, jnp.int32), everyone(), whole, part, (devices, 1, 128), 0
    )[:, 0, 0]
    index = jnp.arange(devices, dtype=jnp.int32)
    starts = jnp.sum(jnp.where(index[None, :] < index[:, None], counts[None, :], 0), axis=1)
    my_start = jnp.sum(jnp.where(index < my_index, counts, 0))
    token_index = jnp.arange(tok_rows, dtype=jnp.int32)
    local_rank = (
        jnp.sum(jnp.where(token_index[None, :] <= token_index[:, None], keep_mask[None, :], 0), axis=1) - 1
    )
    global_rank = my_start + local_rank
    owner = global_rank % devices
    piped = seq_count == 8 and slot_count * ctx_count % 16 == 0
    if piped:
        owner = owner % ctx_count * seq_count + owner // ctx_count
    token_slot = jnp.where(visible, owner * slot_count + local_rank // devices, capacity)
    slot_index = jnp.arange(capacity, dtype=jnp.int32)
    slot_of_token = (token_slot[:, None] == slot_index[None, :]).astype(jnp.bfloat16)
    slot_place = slot_index % slot_count
    source_start = jnp.repeat(starts, slot_count)
    source_count = jnp.repeat(counts, slot_count)
    offset = (my_index - source_start) % devices + devices * slot_place
    usable = offset < source_count
    slot_row = jnp.where(usable, (source_start + offset) // devices, own_rows)
    row_of_slot = (
        slot_row[:, None] == jnp.arange(own_rows, dtype=jnp.int32)[None, :]
    ).astype(jnp.bfloat16)

    embedded = embed(tokens, modality, positions, modal_table)

    def pick(choice, rows, side):
        return lax.dot_general(
            choice, rows, (((side,), (0,)), ((), ())), preferred_element_type=jnp.float32
        )

    normed = layer_norm(embedded, norm_gain, norm_bias)
    outgoing = pick(slot_of_token, normed, 0).astype(jnp.bfloat16)
    slots = (devices, slot_count, feature_width)
    if piped:
        group = spread_rows(outgoing, row_of_slot.T, slot_count, 1)
    else:
        arriving = exchange(outgoing.reshape(slots), everyone(), part, part, slots, 1)
        own_normed = pick(row_of_slot, arriving.reshape(capacity, feature_width), 0).astype(jnp.bfloat16)
        group = exchange(own_normed, along("seq"), whole, part, (seq_count,) + own_normed.shape, 2)
    group = group.reshape(seq_count * own_rows, feature_width)
    triple = jnp.einsum(
        "rd,tdc->trc", group, qkv_weight, preferred_element_type=jnp.float32
    ).astype(jnp.bfloat16)
    if triple.shape[2] % (ctx_count * HEAD_DIM) == 0:
        attended = attend_by_head(triple)
    else:
        attended = attend_by_row(triple)
    if piped:
        returned = return_rows(attended, out_weight, row_of_slot, slot_count, 5)
    else:
        shares = jnp.dot(attended, out_weight, preferred_element_type=jnp.float32).astype(jnp.bfloat16)
        shares = shares.reshape(seq_count, own_rows, feature_width)
        shares = exchange(shares, along("seq"), part, part, shares.shape, 5)
        projected = jnp.sum(shares.astype(jnp.float32), axis=0).astype(jnp.bfloat16)
        returning = pick(row_of_slot, projected, 1).astype(jnp.bfloat16)
        returned = exchange(returning.reshape(slots), everyone(), part, part, slots, 6)
        returned = returned.reshape(capacity, feature_width)
    restored = pick(slot_of_token, returned, 1)
    return jnp.where(visible[:, None], embedded.astype(jnp.float32) + restored, mask_token[None, :])


def solution(mesh):
    in_specs = (
        P(("seq", "ctx"), None),
        P(("seq", "ctx")),
        P(("seq", "ctx")),
        P(("seq", "ctx")),
        P(),
        P(),
        P(),
        P(None, None, "seq"),
        P("seq", None),
        P(),
    )
    out_specs = P(("seq", "ctx"), None)
    return jax.shard_map(local, mesh=mesh, in_specs=in_specs, out_specs=out_specs, check_vma=False)
```

```python
import math

import jax
import jax.numpy as jnp
from jax import lax
from jax.experimental import pallas as pl
from jax.experimental.pallas import tpu as pltpu
from jax.sharding import PartitionSpec as P

HEAD_DIM = 128


EPSILON = 1e-06
MESH = pl.DeviceIdType.MESH


def position_table(positions, feature_width):
    half_width = feature_width // 2
    frequency = jnp.exp(-math.log(10000.0) * jnp.arange(half_width, dtype=jnp.float32) / half_width)
    angles = positions.astype(jnp.float32)[:, None] * frequency[None, :]
    return jnp.concatenate([jnp.sin(angles), jnp.cos(angles)], axis=1)


def embed(tokens, modality, positions, modal_table):
    table_rows = jnp.where(modality[:, None] == 1, modal_table[1][None, :], modal_table[0][None, :])
    summed = tokens.astype(jnp.float32) + position_table(positions, tokens.shape[1]) + table_rows
    return summed.astype(jnp.bfloat16)


def layer_norm(embedded, norm_gain, norm_bias):
    values = embedded.astype(jnp.float32)
    row_mean = jnp.mean(values, axis=1, keepdims=True)
    centered = values - row_mean
    row_var = jnp.mean(centered * centered, axis=1, keepdims=True)
    return (centered * lax.rsqrt(row_var + EPSILON) * norm_gain + norm_bias).astype(jnp.bfloat16)


def everyone():
    seq_count, ctx_count = lax.axis_size("seq"), lax.axis_size("ctx")

    def place():
        return lax.axis_index("seq") * ctx_count + lax.axis_index("ctx")

    return seq_count * ctx_count, place, lambda j: {"seq": j // ctx_count, "ctx": lax.rem(j, ctx_count)}


def along(axis):
    return lax.axis_size(axis), lambda: lax.axis_index(axis), lambda j: {axis: j}


def exchange(x, group, source, target, out_shape, collective_id):
    count, place, device_of = group

    def kernel(x_ref, out_ref, send_sem, recv_sem, own_sem):
        me = place()
        barrier = pltpu.get_barrier_semaphore()

        def greet(step, carry):
            peer = lax.rem(me + step, count)
            pl.semaphore_signal(barrier, inc=1, device_id=device_of(peer), device_id_type=MESH)
            return carry

        def push(step):
            peer = lax.rem(me + step, count)
            return pltpu.make_async_remote_copy(
                src_ref=source(x_ref, peer),
                dst_ref=target(out_ref, me),
                send_sem=send_sem.at[step],
                recv_sem=recv_sem.at[step],
                device_id=device_of(peer),
                device_id_type=MESH,
            )

        def start(step, carry):
            push(step).start()
            return carry

        def finish(step, carry):
            push(step).wait()
            return carry

        lax.fori_loop(1, count, greet, 0)
        own = pltpu.make_async_copy(source(x_ref, me), target(out_ref, me), own_sem)
        own.start()
        pl.semaphore_wait(barrier, count - 1)
        lax.fori_loop(1, count, start, 0)
        lax.fori_loop(1, count, finish, 0)
        own.wait()

    return pl.pallas_call(
        kernel,
        out_shape=jax.ShapeDtypeStruct(out_shape, x.dtype),
        in_specs=[pl.BlockSpec(memory_space=pltpu.VMEM)],
        out_specs=pl.BlockSpec(memory_space=pltpu.VMEM),
        scratch_shapes=[
            pltpu.SemaphoreType.DMA((count,)),
            pltpu.SemaphoreType.DMA((count,)),
            pltpu.SemaphoreType.DMA,
        ],
        compiler_params=pltpu.CompilerParams(collective_id=collective_id, has_side_effects=True),
    )(x)


CHUNKS = 4


def remote(src, dst, sems, at, device):
    send_sem, recv_sem = sems
    return pltpu.make_async_remote_copy(
        src_ref=src,
        dst_ref=dst,
        send_sem=send_sem.at[at],
        recv_sem=recv_sem.at[at],
        device_id=device,
        device_id_type=MESH,
    )


def aligned(start, size):
    return pl.ds(pl.multiple_of(start * size, size), size)


def greet_line_and_plane(seq_count, ctx_count):
    me, level = lax.axis_index("seq"), lax.axis_index("ctx")
    barrier = pltpu.get_barrier_semaphore()
    for step in range(1, seq_count):
        peer = {"seq": lax.rem(me + step, seq_count)}
        pl.semaphore_signal(barrier, inc=1, device_id=peer, device_id_type=MESH)
    for step in range(1, ctx_count):
        peer = {"ctx": lax.rem(level + step, ctx_count)}
        pl.semaphore_signal(barrier, inc=1, device_id=peer, device_id_type=MESH)
    pl.semaphore_wait(barrier, seq_count + ctx_count - 2)


def regrouping(capacity, outer, inner, slot_count):
    row = lax.broadcasted_iota(jnp.int32, (capacity, capacity), 0)
    column = lax.broadcasted_iota(jnp.int32, (capacity, capacity), 1)
    first = row // (inner * slot_count)
    second = row // slot_count % inner
    wanted = (second * outer + first) * slot_count + row % slot_count
    return (column == wanted).astype(jnp.bfloat16)


def moved(choice, rows):
    return jnp.dot(choice, rows, preferred_element_type=jnp.float32).astype(jnp.bfloat16)


def spread_rows(outgoing, choice, qkv_weight, slot_count, collective_id):
    capacity, width = outgoing.shape
    rows = choice.shape[0]
    half = rows // 2
    seq_count, ctx_count = lax.axis_size("seq"), lax.axis_size("ctx")
    line_rows, plane_rows = capacity // ctx_count, capacity // seq_count
    part_width = width // CHUNKS

    kinds, _, local_width = qkv_weight.shape

    def kernel(
        x_ref, choice_ref, w_hbm, triple_ref, mid, ordered, arrived, out_ref, w_ref, total,
        zs, zr, ps, pr, gs, gr, own_sem, own_sems, w_sems,
    ):
        me, level = lax.axis_index("seq"), lax.axis_index("ctx")
        sibling, left, down = flip(me, 1), flip(me, 2), flip(me, 4)
        across = flip(left, 4)
        all_rows, first, second = pl.ds(0, rows), pl.ds(0, half), pl.ds(half, half)
        along_line, over_plane, gathering = (zs, zr), (ps, pr), (gs, gr)

        def cols(k):
            return pl.ds(k * part_width, part_width)

        def line(k, step):
            peer = lax.rem(level + step, ctx_count)
            src = x_ref.at[aligned(peer, line_rows), cols(k)]
            dst = mid.at[aligned(level, line_rows), cols(k)]
            return remote(src, dst, along_line, (k, step), {"ctx": peer})

        def plane(k, step):
            peer = lax.rem(me + step, seq_count)
            src = ordered.at[aligned(peer, plane_rows), cols(k)]
            dst = arrived.at[aligned(me, plane_rows), cols(k)]
            return remote(src, dst, over_plane, (k, step), {"seq": peer})

        def plane_own(k):
            here = aligned(me, plane_rows)
            return pltpu.make_async_copy(ordered.at[here, cols(k)], arrived.at[here, cols(k)], own_sems.at[k])

        moves = (
            (me, all_rows, sibling),
            (me, all_rows, left),
            (me, all_rows, down),
            (left, first, down),
            (down, second, left),
            (left, all_rows, sibling),
            (down, all_rows, sibling),
            (across, first, sibling),
            (across, second, sibling),
        )

        def hand(k, at):
            origin, which, place = moves[at]
            ref = out_ref.at[origin, which, cols(k)]
            return remote(ref, ref, gathering, (k, at), {"seq": place})

        def fetch(k):
            return pltpu.make_async_copy(w_hbm.at[:, cols(k), :], w_ref.at[:, cols(k), :], w_sems.at[k])

        greet_line_and_plane(seq_count, ctx_count)
        for k in range(CHUNKS):
            for step in range(1, ctx_count):
                line(k, step).start()
        for k in range(CHUNKS):
            fetch(k).start()
        here = aligned(level, line_rows)
        own = pltpu.make_async_copy(x_ref.at[here], mid.at[here], own_sem)
        own.start()
        regroup = regrouping(capacity, seq_count, ctx_count, slot_count)
        own.wait()
        for turn in range(CHUNKS + 4):
            k = turn - 4
            if 0 <= k < CHUNKS:
                for at in (0, 5, 6, 7, 8):
                    hand(k, at).wait_recv()
                fetch(k).wait()
                gathered = out_ref[:, :, cols(k)].reshape(seq_count * rows, part_width)
                for kind in range(kinds):
                    term = jnp.dot(gathered, w_ref[kind, cols(k), :], preferred_element_type=jnp.float32)
                    if k == 0:
                        total[kind] = term
                    elif k < CHUNKS - 1:
                        total[kind] += term
                    else:
                        triple_ref[kind] = (total[kind] + term).astype(jnp.bfloat16)
            k = turn - 3
            if 0 <= k < CHUNKS:
                hand(k, 3).wait_recv()
                hand(k, 7).start()
                hand(k, 4).wait_recv()
                hand(k, 8).start()
            k = turn - 2
            if 0 <= k < CHUNKS:
                hand(k, 1).wait_recv()
                hand(k, 3).start()
                hand(k, 5).start()
                hand(k, 2).wait_recv()
                hand(k, 4).start()
                hand(k, 6).start()
            k = turn - 1
            if 0 <= k < CHUNKS:
                for step in range(1, seq_count):
                    plane(k, step).wait_recv()
                plane_own(k).wait()
                out_ref[me, :, cols(k)] = moved(choice_ref[...], arrived[:, cols(k)])
                for at in (1, 2, 0):
                    hand(k, at).start()
            k = turn
            if k < CHUNKS:
                for step in range(1, ctx_count):
                    line(k, step).wait_recv()
                ordered[:, cols(k)] = moved(regroup, mid[:, cols(k)])
                for step in range(1, seq_count):
                    plane(k, step).start()
                plane_own(k).start()
        for k in range(CHUNKS):
            for at in range(9):
                hand(k, at).wait_send()
            for step in range(1, seq_count):
                plane(k, step).wait_send()
            for step in range(1, ctx_count):
                line(k, step).wait_send()

    dma = pltpu.SemaphoreType.DMA
    return pl.pallas_call(
        kernel,
        out_shape=jax.ShapeDtypeStruct((kinds, seq_count * rows, local_width), jnp.bfloat16),
        in_specs=[pl.BlockSpec(memory_space=pltpu.VMEM)] * 2 + [pl.BlockSpec(memory_space=pl.ANY)],
        out_specs=pl.BlockSpec(memory_space=pltpu.VMEM),
        scratch_shapes=[pltpu.VMEM((capacity, width), jnp.bfloat16)] * 3
        + [
            pltpu.VMEM((seq_count, rows, width), jnp.bfloat16),
            pltpu.VMEM(qkv_weight.shape, jnp.bfloat16),
            pltpu.VMEM((kinds, seq_count * rows, local_width), jnp.float32),
        ]
        + [dma((CHUNKS, ctx_count))] * 2
        + [dma((CHUNKS, seq_count))] * 2
        + [dma((CHUNKS, 9))] * 2
        + [dma, dma((CHUNKS,)), dma((CHUNKS,))],
        compiler_params=pltpu.CompilerParams(collective_id=collective_id, has_side_effects=True),
    )(outgoing, choice, qkv_weight)


def flip(position, bit):
    return position + bit * (1 - 2 * lax.rem(position // bit, 2))


def return_rows(attended, out_weight, choice, slot_count, collective_id):
    width = out_weight.shape[1]
    capacity, rows = choice.shape
    half = rows // 2
    seq_count, ctx_count = lax.axis_size("seq"), lax.axis_size("ctx")
    line_rows, plane_rows = capacity // ctx_count, capacity // seq_count
    part_width = width // CHUNKS

    def kernel(
        x_ref, w_ref, choice_ref, out_ref, shares, near, sums, from_left, from_down, last, passed, total,
        sorted_rows, arrived, ordered, ss, sr, ps, pr, zs, zr, own_sems, line_sems,
    ):
        me, level = lax.axis_index("seq"), lax.axis_index("ctx")
        sibling, left, down = flip(me, 1), flip(me, 2), flip(me, 4)
        first, second = pl.ds(0, half), pl.ds(half, half)
        summing, over_plane, along_line = (ss, sr), (ps, pr), (zs, zr)

        def cols(k):
            return pl.ds(k * part_width, part_width)

        def at(place, which):
            place = flip(place, 2) if which % 2 else place
            return flip(place, 4) if which // 2 else place

        def over(k, q):
            src = shares.at[aligned(at(sibling, q), rows), cols(k)]
            return remote(src, near.at[q, :, cols(k)], summing, (k, q), {"seq": sibling})

        def far(k, which):
            if which == 0:
                return remote(sums.at[3, first, cols(k)], from_left.at[1, :, cols(k)], summing, (k, 4), {"seq": left})
            if which == 1:
                return remote(sums.at[3, second, cols(k)], from_down.at[1, :, cols(k)], summing, (k, 5), {"seq": down})
            if which == 2:
                return remote(sums.at[1, first, cols(k)], from_left.at[0, :, cols(k)], summing, (k, 6), {"seq": left})
            if which == 3:
                return remote(sums.at[2, second, cols(k)], from_down.at[0, :, cols(k)], summing, (k, 7), {"seq": down})
            if which == 4:
                return remote(passed.at[0, :, cols(k)], last.at[0, :, cols(k)], summing, (k, 8), {"seq": down})
            return remote(passed.at[1, :, cols(k)], last.at[1, :, cols(k)], summing, (k, 9), {"seq": left})

        def plane(k, step):
            peer = lax.rem(me + step, seq_count)
            src = sorted_rows.at[aligned(peer, plane_rows), cols(k)]
            dst = arrived.at[aligned(me, plane_rows), cols(k)]
            return remote(src, dst, over_plane, (k, step), {"seq": peer})

        def plane_own(k):
            here = aligned(me, plane_rows)
            return pltpu.make_async_copy(sorted_rows.at[here, cols(k)], arrived.at[here, cols(k)], own_sems.at[k])

        def line(k, step):
            peer = lax.rem(level + step, ctx_count)
            src = ordered.at[aligned(peer, line_rows), cols(k)]
            dst = out_ref.at[aligned(level, line_rows), cols(k)]
            return remote(src, dst, along_line, (k, step), {"ctx": peer})

        def line_own(k):
            here = aligned(level, line_rows)
            return pltpu.make_async_copy(ordered.at[here, cols(k)], out_ref.at[here, cols(k)], line_sems.at[k])

        def wide(value):
            return value.astype(jnp.float32)

        def narrow(value):
            return value.astype(jnp.bfloat16)

        greet_line_and_plane(seq_count, ctx_count)
        regroup = regrouping(capacity, ctx_count, seq_count, slot_count)
        order = (3, 1, 2, 0)
        for turn in range(CHUNKS + 4):
            k = turn - 4
            if 0 <= k < CHUNKS:
                for step in range(1, seq_count):
                    plane(k, step).wait_recv()
                plane_own(k).wait()
                ordered[:, cols(k)] = moved(regroup, arrived[:, cols(k)])
                for step in range(1, ctx_count):
                    line(k, step).start()
                line_own(k).start()
            k = turn - 3
            if 0 <= k < CHUNKS:
                c = cols(k)
                far(k, 2).wait_recv()
                far(k, 4).wait_recv()
                total[:half, c] = narrow(wide(sums[0, :half, c]) + wide(from_left[0, :, c]) + wide(last[0, :, c]))
                far(k, 3).wait_recv()
                far(k, 5).wait_recv()
                total[half:, c] = narrow(wide(sums[0, half:, c]) + wide(from_down[0, :, c]) + wide(last[1, :, c]))
                sorted_rows[:, c] = moved(choice_ref[...], total[:, c])
                for step in range(1, seq_count):
                    plane(k, step).start()
                plane_own(k).start()
            k = turn - 2
            if 0 <= k < CHUNKS:
                c = cols(k)
                far(k, 0).wait_recv()
                passed[0, :, c] = narrow(wide(sums[2, :half, c]) + wide(from_left[1, :, c]))
                far(k, 4).start()
                far(k, 1).wait_recv()
                passed[1, :, c] = narrow(wide(sums[1, half:, c]) + wide(from_down[1, :, c]))
                far(k, 5).start()
            k = turn - 1
            if 0 <= k < CHUNKS:
                c = cols(k)
                for q in order:
                    over(k, q).wait_recv()
                    mine = shares[aligned(at(me, q), rows), c]
                    sums[q, :, c] = narrow(wide(mine) + wide(near[q, :, c]))
                    if q == 3:
                        far(k, 0).start()
                        far(k, 1).start()
                    if q == 1:
                        far(k, 2).start()
                    if q == 2:
                        far(k, 3).start()
            k = turn
            if k < CHUNKS:
                shares[:, cols(k)] = moved(x_ref[...], w_ref[:, cols(k)])
                for q in order:
                    over(k, q).start()
        for k in range(CHUNKS):
            for step in range(1, ctx_count):
                line(k, step).wait()
            line_own(k).wait()
            for step in range(1, seq_count):
                plane(k, step).wait_send()
            for q in order:
                over(k, q).wait_send()
            for which in range(6):
                far(k, which).wait_send()

    dma = pltpu.SemaphoreType.DMA
    bf16 = jnp.bfloat16
    return pl.pallas_call(
        kernel,
        out_shape=jax.ShapeDtypeStruct((capacity, width), bf16),
        in_specs=[pl.BlockSpec(memory_space=pltpu.VMEM)] * 3,
        out_specs=pl.BlockSpec(memory_space=pltpu.VMEM),
        scratch_shapes=[pltpu.VMEM((seq_count * rows, width), bf16)]
        + [pltpu.VMEM((4, rows, width), bf16)] * 2
        + [pltpu.VMEM((2, half, width), bf16)] * 4
        + [pltpu.VMEM((rows, width), bf16)]
        + [pltpu.VMEM((capacity, width), bf16)] * 3
        + [dma((CHUNKS, 10))] * 2
        + [dma((CHUNKS, seq_count))] * 2
        + [dma((CHUNKS, ctx_count))] * 2
        + [dma((CHUNKS,))] * 2,
        compiler_params=pltpu.CompilerParams(collective_id=collective_id, has_side_effects=True),
    )(attended, out_weight, choice)


def part(ref, j):
    return ref.at[j]


def whole(ref, j):
    return ref


def attend(triple):
    _, heads, rows, _ = triple.shape
    block = min(rows, 256)
    score_scale = 1.0 / math.sqrt(HEAD_DIM)

    def kernel(q_ref, k_ref, v_ref, out_ref):
        scores = (
            lax.dot_general(
                q_ref[...], k_ref[...], (((1,), (1,)), ((), ())), preferred_element_type=jnp.float32
            )
            * score_scale
        )
        expanded = jnp.exp(scores - jnp.max(scores, axis=1, keepdims=True))
        total = jnp.sum(expanded, axis=1, keepdims=True)
        summed = jnp.dot(expanded.astype(jnp.bfloat16), v_ref[...], preferred_element_type=jnp.float32)
        out_ref[...] = (summed / total).astype(jnp.bfloat16)

    return pl.pallas_call(
        kernel,
        grid=(heads, rows // block),
        out_shape=jax.ShapeDtypeStruct((heads, rows, HEAD_DIM), jnp.bfloat16),
        in_specs=[
            pl.BlockSpec((None, None, block, HEAD_DIM), lambda h, i: (0, h, i, 0)),
            pl.BlockSpec((None, None, rows, HEAD_DIM), lambda h, i: (1, h, 0, 0)),
            pl.BlockSpec((None, None, rows, HEAD_DIM), lambda h, i: (2, h, 0, 0)),
        ],
        out_specs=pl.BlockSpec((None, block, HEAD_DIM), lambda h, i: (h, i, 0)),
    )(triple, triple, triple)


def attend_by_head(triple):
    _, group_rows, local_width = triple.shape
    ctx = along("ctx")
    count = ctx[0]
    width = local_width // count
    heads = width // HEAD_DIM
    gathered = exchange(
        triple,
        ctx,
        lambda ref, j: ref.at[:, :, pl.ds(pl.multiple_of(j * width, HEAD_DIM), width)],
        lambda ref, j: ref.at[:, pl.ds(pl.multiple_of(j * group_rows, group_rows), group_rows), :],
        (3, count * group_rows, width),
        3,
    )
    if heads == 1:
        split = gathered[:, None]
    else:
        split = jnp.transpose(
            gathered.reshape(3, count * group_rows, heads, HEAD_DIM), (0, 2, 1, 3)
        )
    done = attend(split)
    if heads == 1:
        done = done[0]
    else:
        done = jnp.transpose(done, (1, 0, 2)).reshape(count * group_rows, width)
    return exchange(
        done,
        ctx,
        lambda ref, j: ref.at[pl.ds(pl.multiple_of(j * group_rows, group_rows), group_rows), :],
        lambda ref, j: ref.at[:, pl.ds(pl.multiple_of(j * width, HEAD_DIM), width)],
        (group_rows, local_width),
        4,
    )


def attend_by_row(triple):
    queries, key_rows, values = (triple[0], triple[1], triple[2])
    group_rows, local_width = queries.shape
    heads_here = local_width // HEAD_DIM
    score_scale = 1.0 / math.sqrt(HEAD_DIM)
    both = lax.all_gather(jnp.stack([key_rows, values]), "ctx", axis=1, tiled=True)
    length = both.shape[1]
    query_heads = queries.reshape(group_rows, heads_here, HEAD_DIM)
    key_heads = both[0].reshape(length, heads_here, HEAD_DIM)
    value_heads = both[1].reshape(length, heads_here, HEAD_DIM)
    scores = (
        jnp.einsum("ghd,khd->hgk", query_heads, key_heads, preferred_element_type=jnp.float32)
        * score_scale
    )
    expanded = jnp.exp(scores - jnp.max(scores, axis=2, keepdims=True))
    total = jnp.sum(expanded, axis=2, keepdims=True)
    summed = jnp.einsum(
        "hgk,khd->hgd",
        expanded.astype(jnp.bfloat16),
        value_heads,
        preferred_element_type=jnp.float32,
    )
    attended = (summed / total).astype(jnp.bfloat16)
    return jnp.transpose(attended, (1, 0, 2)).reshape(group_rows, local_width)


def local(
    tokens,
    modality,
    keep_mask,
    positions,
    modal_table,
    norm_gain,
    norm_bias,
    qkv_weight,
    out_weight,
    mask_token,
):
    tok_rows, feature_width = tokens.shape
    seq_count = lax.axis_size("seq")
    ctx_count = lax.axis_size("ctx")
    devices = seq_count * ctx_count
    slot_count = (tok_rows + devices - 1) // devices
    capacity = devices * slot_count
    own_rows = tok_rows // 4
    my_index = lax.axis_index("seq") * ctx_count + lax.axis_index("ctx")
    visible = keep_mask == 1
    own_count = jnp.sum(keep_mask)
    counts = exchange(
        jnp.full((1, 128), own_count, jnp.int32), everyone(), whole, part, (devices, 1, 128), 0
    )[:, 0, 0]
    index = jnp.arange(devices, dtype=jnp.int32)
    starts = jnp.sum(jnp.where(index[None, :] < index[:, None], counts[None, :], 0), axis=1)
    my_start = jnp.sum(jnp.where(index < my_index, counts, 0))
    token_index = jnp.arange(tok_rows, dtype=jnp.int32)
    local_rank = (
        jnp.sum(jnp.where(token_index[None, :] <= token_index[:, None], keep_mask[None, :], 0), axis=1) - 1
    )
    global_rank = my_start + local_rank
    owner = global_rank % devices
    piped = seq_count == 8 and slot_count * ctx_count % 16 == 0
    if piped:
        owner = owner % ctx_count * seq_count + owner // ctx_count
    token_slot = jnp.where(visible, owner * slot_count + local_rank // devices, capacity)
    slot_index = jnp.arange(capacity, dtype=jnp.int32)
    slot_of_token = (token_slot[:, None] == slot_index[None, :]).astype(jnp.bfloat16)
    slot_place = slot_index % slot_count
    source_start = jnp.repeat(starts, slot_count)
    source_count = jnp.repeat(counts, slot_count)
    offset = (my_index - source_start) % devices + devices * slot_place
    usable = offset < source_count
    slot_row = jnp.where(usable, (source_start + offset) // devices, own_rows)
    row_of_slot = (
        slot_row[:, None] == jnp.arange(own_rows, dtype=jnp.int32)[None, :]
    ).astype(jnp.bfloat16)

    embedded = embed(tokens, modality, positions, modal_table)

    def pick(choice, rows, side):
        return lax.dot_general(
            choice, rows, (((side,), (0,)), ((), ())), preferred_element_type=jnp.float32
        )

    normed = layer_norm(embedded, norm_gain, norm_bias)
    outgoing = pick(slot_of_token, normed, 0).astype(jnp.bfloat16)
    slots = (devices, slot_count, feature_width)
    if piped:
        triple = spread_rows(outgoing, row_of_slot.T, qkv_weight, slot_count, 1)
    else:
        arriving = exchange(outgoing.reshape(slots), everyone(), part, part, slots, 1)
        own_normed = pick(row_of_slot, arriving.reshape(capacity, feature_width), 0).astype(jnp.bfloat16)
        group = exchange(own_normed, along("seq"), whole, part, (seq_count,) + own_normed.shape, 2)
        triple = jnp.einsum(
            "rd,tdc->trc",
            group.reshape(seq_count * own_rows, feature_width),
            qkv_weight,
            preferred_element_type=jnp.float32,
        ).astype(jnp.bfloat16)
    if triple.shape[2] % (ctx_count * HEAD_DIM) == 0:
        attended = attend_by_head(triple)
    else:
        attended = attend_by_row(triple)
    if piped:
        returned = return_rows(attended, out_weight, row_of_slot, slot_count, 5)
    else:
        shares = jnp.dot(attended, out_weight, preferred_element_type=jnp.float32).astype(jnp.bfloat16)
        shares = shares.reshape(seq_count, own_rows, feature_width)
        shares = exchange(shares, along("seq"), part, part, shares.shape, 5)
        projected = jnp.sum(shares.astype(jnp.float32), axis=0).astype(jnp.bfloat16)
        returning = pick(row_of_slot, projected, 1).astype(jnp.bfloat16)
        returned = exchange(returning.reshape(slots), everyone(), part, part, slots, 6)
        returned = returned.reshape(capacity, feature_width)
    restored = pick(slot_of_token, returned, 1)
    return jnp.where(visible[:, None], embedded.astype(jnp.float32) + restored, mask_token[None, :])


def solution(mesh):
    in_specs = (
        P(("seq", "ctx"), None),
        P(("seq", "ctx")),
        P(("seq", "ctx")),
        P(("seq", "ctx")),
        P(),
        P(),
        P(),
        P(None, None, "seq"),
        P("seq", None),
        P(),
    )
    out_specs = P(("seq", "ctx"), None)
    return jax.shard_map(local, mesh=mesh, in_specs=in_specs, out_specs=out_specs, check_vma=False)
```
